32 devices in a mesh: groups: 2 (over y), ctx: 4 (over x, core), chan: 4 (over z).
Axes of the slice: x: 2, y: 2, z: 4, core: 2. Of those that a mesh axis runs over, the one named last changes fastest.
Arguments:
- stream: bfloat16 [1536, 4096], P(('groups', 'ctx'), 'chan'), parts along dimension 0, may hold values from -30 to 30
- in_weights: bfloat16 [2, 4096, 3, 2048], P(None, 'ctx', None, 'chan'), may hold values from -0.09375 to 0.09375
- out_weights: bfloat16 [2, 4096, 2048], P(None, 'ctx', 'chan'), may hold values from -0.125 to 0.125
- short_taps: bfloat16 [7, 2048], P(None, 'chan'), may hold values from -2.390625 to 2.390625
- medium_taps: bfloat16 [128, 128], P(None, 'chan'), may hold values from -0.5390625 to 0.5390625
- plan: int32 [4], replicated, may hold values from 0 to 1
Outputs:
- result: bfloat16 [1536, 4096], P(('groups', 'ctx'), 'chan'), parts along dimension 0
The draws below stay inside these ranges and needn't reach their ends.
There are 2 independent parts, one for each index of `groups`. The reference program is written for one: setup_inputs(seed, part) draws one part's arguments, and reference() takes and returns one part's arrays. A program takes and returns all parts, laid end to end along the dimension named above; an argument that names none is the same for every part. Nothing has to cross between parts.
All inputs are finite; a program needn't handle non-finite values.
Results may differ from the reference program's by a relative error of at most 0.03.
Values may be sent and summed in bfloat16 or wider, within the bound.
A program may use at most 128 MiB of HBM per device.

```python
import jax
import jax.numpy as jnp
from jax import lax

D = 4096
C = 2048
SHORT_TAPS = 7
MEDIUM_TAPS = 128
STEPS = 4
TOKENS = 768
GROUPS = 128
N_CHAN = 4


def draw_stream(key, part):
    key_list = jax.random.split(key, 4)
    row_scale = jnp.exp(jax.random.uniform(key_list[0], (TOKENS, 1), jnp.float32, jnp.log(0.3), jnp.log(3.0)))
    col_scale = jnp.exp(jax.random.uniform(key_list[1], (1, D), jnp.float32, jnp.log(0.3), jnp.log(3.0)))
    base_noise = jax.random.truncated_normal(key_list[3], -4.0, 4.0, (TOKENS, D), jnp.float32)
    return jnp.clip(base_noise * row_scale * col_scale, -30.0, 30.0).astype(jnp.bfloat16)


def with_ends(drawn, rng, low, high):
    place = [jax.random.randint(jax.random.fold_in(rng, axis), (), 0, length) for axis, length in enumerate(drawn.shape)]
    main_axis = drawn.shape.index(max(drawn.shape))
    beside = place[:main_axis] + [(place[main_axis] + 1) % drawn.shape[main_axis]] + place[main_axis + 1:]
    return drawn.at[tuple(place)].set(low).at[tuple(beside)].set(high)


def block_scale(stream_key, dims, shards, low, top_value):
    def one(dim, parts):
        heights = jax.random.uniform(jax.random.fold_in(jax.random.fold_in(stream_key, 6), dim), (parts,), jnp.float32, low / len(shards), top_value / len(shards))
        return jnp.repeat(jnp.exp(heights), dims[dim] // parts).reshape((-1,) + (1,) * (len(dims) - dim - 1))

    level = one(*shards[0])
    for cut in shards[1:]:
        level = level * one(*cut)
    return level


def bell_draw(key, extent, width, limit, pieces=(), kind=jnp.bfloat16):
    entries = jax.random.normal(key, extent, jnp.float32) * width
    if len(pieces) > 0:
        entries = block_scale(key, extent, pieces, -0.22, 0.18) * entries
    return jnp.clip(entries, min=-limit, max=limit).astype(kind)


def setup_inputs(seed: int = 0, part: int = 0) -> dict:
    seeds = jax.random.split(jax.random.key(seed), 7)
    own_keys = jax.random.split(jax.random.fold_in(seeds[6], part), 7)
    stream = draw_stream(jax.random.fold_in(jax.random.fold_in(seeds[6], part), 71), part)
    in_weights = bell_draw(seeds[1], (2, D, 3, C), D ** -0.5, 0.09375, ((1, 4), (3, 4)))
    out_weights = bell_draw(seeds[2], (2, D, C), C ** -0.5, 0.125, ((1, 4), (2, 4)))
    short_taps = bell_draw(seeds[3], (SHORT_TAPS, C), 0.4, 2.390625, ((1, 4),))
    medium_taps = bell_draw(seeds[4], (MEDIUM_TAPS, GROUPS), 0.09, 0.5390625, ((1, 4),))
    plan = with_ends(jax.random.randint(seeds[5], (STEPS,), 0, 2), jax.random.fold_in(seeds[5], 1), 0, 1).astype(jnp.int32)
    return {"stream": stream, "in_weights": in_weights, "out_weights": out_weights, "short_taps": short_taps, "medium_taps": medium_taps, "plan": plan}


def section_taps(section, short_taps, medium_taps):
    reach = medium_taps.shape[0]
    channels = short_taps.shape[1]
    padding = jnp.zeros((reach - short_taps.shape[0], channels), short_taps.dtype)
    short_full = jnp.concatenate([short_taps, padding], 0)
    group_size = channels // medium_taps.shape[1]
    medium_full = jnp.broadcast_to(medium_taps[:, :, None], (reach, medium_taps.shape[1], group_size)).reshape(reach, channels)
    return jnp.where(section == 0, short_full, medium_full)

def causal_filter(extended, filter_taps):
    reach = filter_taps.shape[0]
    length = extended.shape[0] - reach + 1
    taps_wide = filter_taps.astype(jnp.float32)

    def add_tap(tap_index, total):
        index_now = jnp.asarray(tap_index).astype(jnp.int32)
        start = (jnp.int32(reach - 1) - index_now).astype(jnp.int32)
        window = lax.dynamic_slice_in_dim(extended, start, length, 0).astype(jnp.float32)
        weight_row = lax.dynamic_index_in_dim(taps_wide, index_now, 0, keepdims=True)
        return total + weight_row * window
    start_total = jnp.zeros((length, extended.shape[1]), jnp.float32)
    return lax.fori_loop(0, reach, add_tap, start_total)

def reference(stream, in_weights, out_weights, short_taps, medium_taps, plan):
    hidden = stream
    tokens = stream.shape[0]
    block_width = C // N_CHAN
    for step_index in range(STEPS):
        section = plan[step_index]
        weight_in = lax.dynamic_index_in_dim(in_weights, section, 0, keepdims=False)
        weight_out = lax.dynamic_index_in_dim(out_weights, section, 0, keepdims=False)
        widened = hidden.astype(jnp.float32)
        row_scale = lax.rsqrt(lax.optimization_barrier(jnp.mean(widened * widened, axis=1, keepdims=True)) + 1e-05)
        projected = jnp.dot(hidden, weight_in.reshape(D, 3 * C), preferred_element_type=jnp.float32)
        projected = projected.reshape(tokens, 3, C) * row_scale[:, :, None]
        query_bf = projected[:, 0].astype(jnp.bfloat16)
        mixed_bf = (projected[:, 1] * projected[:, 2]).astype(jnp.bfloat16)
        history = jnp.zeros((MEDIUM_TAPS - 1, C), jnp.bfloat16)
        filtered = causal_filter(jnp.concatenate([history, mixed_bf], 0), section_taps(section, short_taps, medium_taps))
        gated_bf = (query_bf.astype(jnp.float32) * filtered).astype(jnp.bfloat16)
        update = jnp.zeros((tokens, D), jnp.float32)
        for block_index in range(N_CHAN):
            lower = block_index * block_width
            block_term = lax.dot_general(gated_bf[:, lower:lower + block_width], weight_out[:, lower:lower + block_width], (((1,), (1,)), ((), ())), preferred_element_type=jnp.float32)
            update = update + lax.optimization_barrier(block_term.astype(jnp.bfloat16)).astype(jnp.float32)
        hidden = (hidden.astype(jnp.float32) + update).astype(jnp.bfloat16)
    return hidden
```

```python
from functools import partial

import jax
import jax.numpy as jnp
from jax import lax
from jax.experimental import pallas as pl
from jax.experimental.pallas import tpu as pltpu
from jax.sharding import PartitionSpec as P

STEPS = 4


def passed_along(value, axis, steps):
    count = lax.axis_size(axis)
    leading, last = (max(0, -steps), min(count, count - steps))
    return lax.ppermute(value, axis, [(source, source + steps) for source in range(leading, last)])


def section_taps(section, short_taps, medium_taps):
    reach = medium_taps.shape[0]
    channels = short_taps.shape[1]
    padding = jnp.zeros((reach - short_taps.shape[0], channels), short_taps.dtype)
    short_full = jnp.concatenate([short_taps, padding], 0)
    group_size = channels // medium_taps.shape[1]
    medium_full = jnp.broadcast_to(
        medium_taps[:, :, None], (reach, medium_taps.shape[1], group_size)
    ).reshape(reach, channels)
    return jnp.where(section == 0, short_full, medium_full)


def causal_filter(extended, filter_taps):
    filtered = lax.conv_general_dilated(
        extended[None],
        filter_taps[::-1][:, None, :],
        (1,),
        "VALID",
        dimension_numbers=("NWC", "WIO", "NWC"),
        feature_group_count=filter_taps.shape[1],
        preferred_element_type=jnp.float32,
    )
    return filtered[0]


def filter_gate(projected, section, short_taps, medium_taps):
    query_bf = projected[:, 0].astype(jnp.bfloat16)
    mixed_bf = (projected[:, 1] * projected[:, 2]).astype(jnp.bfloat16)
    reach = medium_taps.shape[0]
    earlier = passed_along(mixed_bf[-reach:], "ctx", 1)
    extended = jnp.concatenate([earlier[1:], mixed_bf], 0)
    filtered = causal_filter(extended, section_taps(section, short_taps, medium_taps))
    return (query_bf.astype(jnp.float32) * filtered).astype(jnp.bfloat16)


def expand_rows(hidden):
    return lax.all_gather(hidden, "chan", axis=1, tiled=True)


def combine(hidden, partial_sum):
    update = lax.psum_scatter(
        partial_sum.astype(jnp.bfloat16), "chan", scatter_dimension=1, tiled=True
    ).astype(jnp.float32)
    return (hidden.astype(jnp.float32) + update).astype(jnp.bfloat16)


def advance(hidden, section, project, emit, short_taps, medium_taps):
    full_rows = expand_rows(hidden)
    widened = full_rows.astype(jnp.float32)
    row_scale = lax.rsqrt(jnp.mean(widened * widened, axis=1, keepdims=True) + 1e-05)
    projected, kept_in = project(full_rows, section)
    projected = projected.reshape(full_rows.shape[0], 3, -1) * row_scale[:, :, None]
    gated_bf = filter_gate(projected, section, short_taps, medium_taps)
    partial_sum, kept_out = emit(gated_bf, section)
    return (combine(hidden, partial_sum), kept_in, kept_out)


def stored_project(weights_in, full_rows, section):
    chosen = lax.dynamic_index_in_dim(weights_in, section, 0, keepdims=False)
    projected = jnp.dot(
        full_rows, chosen.reshape(chosen.shape[0], -1), preferred_element_type=jnp.float32
    )
    return (projected, weights_in)


def stored_emit(weights_out, gated_bf, section):
    chosen = lax.dynamic_index_in_dim(weights_out, section, 0, keepdims=False)
    product = lax.dot_general(
        gated_bf, chosen, (((1,), (1,)), ((), ())), preferred_element_type=jnp.float32
    )
    return (product, weights_out)


def shards(stream, in_weights, out_weights, short_taps, medium_taps, plan):
    hidden = stream
    weights_in, weights_out = (
        lax.all_gather(in_weights, "ctx", axis=1, tiled=True),
        lax.all_gather(out_weights, "ctx", axis=1, tiled=True),
    )
    first_step = 0
    for step_index in range(first_step, STEPS):
        hidden, weights_in, weights_out = advance(
            hidden,
            plan[step_index],
            partial(stored_project, weights_in),
            partial(stored_emit, weights_out),
            short_taps,
            medium_taps,
        )
    return hidden


CHUNKS = 12
CROSS, MIX, EMIT, DOT, MEET, UPDATE, ARRIVE = 1, 3, 4, 5, 7, 9, 12
PAD = 128
LANES = 128
BF = jnp.bfloat16
F32 = jnp.float32


def wave_kernel(
    sizes, plan, stream, w_in, w_out, taps, out,
    h, land, p_send, p_recv, x_send, x_recv, own, ss_own, ss_recv, mixed, gat, acc, r_send, r_recv, c_recv,
    i_r, up_s, down_s, m_s, m_r, ss_s, ss_r, p_s, p_r, x_s, x_r, g_s, g_r, r_s, r_r, c_s, c_r, b_s, b_r, o_s, o_r,
):
    tokens, rows, block, width = sizes
    ctx, chan = lax.axis_index("ctx"), lax.axis_index("chan")
    n_ctx, n_chan = 4, 4
    side, core = ctx // 2, ctx % 2
    partner = {"ctx": side * 2 + (1 - core)}
    across = {"ctx": (1 - side) * 2 + core}
    diagonal = {"ctx": (1 - side) * 2 + (1 - core)}
    relations = (partner, across, diagonal)
    last = n_chan - 1
    outer = (chan == 0) | (chan == last)
    inner = jnp.logical_not(outer)
    near = {"chan": chan + 1 - 2 * (chan % 2)}
    mid = {"chan": jnp.where(outer, near["chan"], last - chan)}
    above = {"chan": jnp.minimum(chan + 1, last)}
    below = {"chan": jnp.maximum(chan - 1, 0)}
    corner = ctx == chan
    items = STEPS * CHUNKS
    each_block = CHUNKS // n_ctx

    def remote(source, target, send, recv, device):
        return pltpu.make_async_remote_copy(
            src_ref=source, dst_ref=target, send_sem=send, recv_sem=recv,
            device_id=device, device_id_type=pl.DeviceIdType.MESH,
        )

    def span(t):
        return pl.ds(pl.multiple_of(t * rows, rows), rows)

    def lanes(index):
        return pl.ds(pl.multiple_of(index * LANES, LANES), LANES)

    def each(count, body):
        def wrapped(t, carry):
            body(t)
            return carry
        lax.fori_loop(0, count, wrapped, 0)

    barrier = pltpu.get_barrier_semaphore()
    for di in range(n_ctx):
        for dk in range(n_chan):
            if di or dk:
                pl.semaphore_signal(
                    barrier, inc=1,
                    device_id={"ctx": (ctx + di) % n_ctx, "chan": (chan + dk) % n_chan},
                    device_id_type=pl.DeviceIdType.MESH,
                )
    pl.semaphore_wait(barrier, n_ctx * n_chan - 1)

    def hop_copy(source, q, j, upward):
        sems, device = (up_s, above) if upward else (down_s, below)
        return remote(source, land.at[q, span(j), :], sems.at[q, j], i_r.at[q, j], device)

    def spread_copy(source, q, j):
        chunk = ctx * each_block + j
        return remote(source, h.at[span(chunk), :], m_s.at[q, j], m_r.at[chunk], {"ctx": q})

    def keep_copy(source, j):
        chunk = ctx * each_block + j
        return pltpu.make_async_copy(source, h.at[span(chunk), :], m_r.at[chunk])

    def spread(source, q, j):
        @pl.when(q != ctx)
        def _():
            spread_copy(source, q, j).start()

        @pl.when(q == ctx)
        def _():
            keep_copy(source, j).start()

    def first(j):
        source = stream.at[span(j), :]

        @pl.when(chan < last)
        def _():
            hop_copy(source, chan, j, True).start()

        @pl.when(chan > 0)
        def _():
            hop_copy(source, chan, j, False).start()

        spread(source, chan, j)

    def relay(j):
        for distance in range(1, n_chan):
            @pl.when(chan >= distance)
            def _():
                q = chan - distance
                source = land.at[q, span(j), :]
                hop_copy(source, q, j, True).wait_recv()

                @pl.when(chan < last)
                def _():
                    hop_copy(source, q, j, True).start()

                spread(source, q, j)

            @pl.when(chan + distance <= last)
            def _():
                q = chan + distance
                source = land.at[q, span(j), :]
                hop_copy(source, q, j, False).wait_recv()

                @pl.when(chan > 0)
                def _():
                    hop_copy(source, q, j, False).start()

                spread(source, q, j)

    def relay_settle(j):
        for q in range(n_chan):
            source = land.at[q, span(j), :]

            @pl.when((q <= chan) & (chan < last))
            def _():
                hop_copy(source, q, j, True).wait_send()

            @pl.when((q >= chan) & (chan > 0))
            def _():
                hop_copy(source, q, j, False).wait_send()

            @pl.when(q != ctx)
            def _():
                spread_copy(source, q, j).wait_send()

    def first_arrive(t):
        @pl.when(t // each_block == ctx)
        def _():
            pltpu.make_async_copy(stream.at[span(0), :], h.at[span(t), :], m_r.at[t]).wait()

        @pl.when(t // each_block != ctx)
        def _():
            remote(stream.at[span(0), :], h.at[span(t), :], m_s.at[0, 0], m_r.at[t], partner).wait_recv()

    def ss_copy(rel, t):
        return remote(ss_own.at[t], ss_recv.at[rel, t], ss_s.at[rel, t], ss_r.at[rel, t], relations[rel])

    def p_copy(slot, t):
        return remote(p_send.at[slot, t], p_recv.at[slot, t], p_s.at[slot, t], p_r.at[slot, t], partner)

    def x_copy(t):
        return remote(x_send.at[t], x_recv.at[t], x_s.at[t], x_r.at[t], across)

    def g_copy(kind, t, sending=True):
        owner = (1 - side) * 2 + core if kind == 2 else ctx
        if not sending:
            owner = (across["ctx"], partner["ctx"], diagonal["ctx"])[kind]
        ref = gat.at[span(t), lanes(owner)]
        return remote(ref, ref, g_s.at[kind, t], g_r.at[kind, t], across if kind == 0 else partner)

    def r_copy(t):
        return remote(r_send.at[t], r_recv.at[t], r_s.at[t], r_r.at[t], near)

    def c_copy(parity, t):
        return remote(r_send.at[t], c_recv.at[parity, t], c_s.at[parity, t], c_r.at[parity, t], mid)

    def b_copy(t):
        ref = h.at[span(t), :]
        return remote(ref, ref, b_s.at[t], b_r.at[t], near)

    home = side == chan // 2

    def gives(s):
        return inner & ((s + 1 < STEPS) | jnp.logical_not(home))

    def takes(s):
        return inner & ((s + 1 < STEPS) | home)

    def returns(s):
        return inner & ((s + 1 < STEPS) | (ctx == near["chan"]))

    def awaits(s):
        return outer & ((s + 1 < STEPS) | corner)

    def settle(s, t):
        for slot in range(2):
            p_copy(slot, t).wait_send()
        for rel in range(3):
            ss_copy(rel, t).wait_send()
        x_copy(t).wait_send()
        for kind in range(3):
            g_copy(kind, t).wait_send()

        @pl.when(outer)
        def _():
            r_copy(t).wait_send()

        @pl.when(gives(s))
        def _():
            c_copy(s % 2, t).wait_send()

        @pl.when(returns(s))
        def _():
            b_copy(t).wait_send()

    def project(section, t, index):
        columns = lanes(index)
        weights = jnp.concatenate([w_in[section, j, :, columns] for j in range(3)], 1)
        return jnp.dot(h[span(t), :], weights, preferred_element_type=F32)

    def enter(s, t):
        section = plan[s]

        @pl.when(s > 0)
        def _():
            settle(s - 1, t)

            @pl.when(outer)
            def _():
                b_copy(t).wait_recv()

        @pl.when(s == 0)
        def _():
            first_arrive(t)

        p_send[0, t] = project(section, t, diagonal["ctx"]).astype(BF)
        p_copy(0, t).start()
        p_send[1, t] = project(section, t, partner["ctx"]).astype(BF)
        p_copy(1, t).start()
        wide = h[span(t), :].astype(F32)
        squares = (wide * wide).astype(BF)
        ss_own[t, :, pl.ds(0, rows)] = lax.dot_general(
            jnp.ones((8, squares.shape[1]), BF), squares, (((1,), (1,)), ((), ())), preferred_element_type=F32
        )
        for rel in range(3):
            ss_copy(rel, t).start()

    def cross(s, t):
        section = plan[s]
        passing = project(section, t, across["ctx"])
        p_copy(0, t).wait_recv()
        x_send[t] = (passing + p_recv[0, t].astype(F32)).astype(BF)
        x_copy(t).start()
        own[t] = project(section, t, ctx)

    def mix(s, t):
        section = plan[s]
        for rel in range(3):
            ss_copy(rel, t).wait_recv()
        p_copy(1, t).wait_recv()
        x_copy(t).wait_recv()
        total = ss_own[t] + ss_recv[0, t] + ss_recv[1, t] + ss_recv[2, t]
        scale = lax.rsqrt(total * (1.0 / width) + 1e-05)
        scale = jnp.transpose(scale)[:rows, :1]
        parts = (own[t] + p_recv[1, t].astype(F32) + x_recv[t].astype(F32)) * scale
        query = parts[:, :LANES].astype(BF).astype(F32)
        product = parts[:, LANES:2 * LANES] * parts[:, 2 * LANES:]
        mixed[pl.ds(pl.multiple_of(PAD + t * rows, rows), rows), :] = product.astype(BF).astype(F32)

        def tap_block(jj, total):
            start = pl.multiple_of(PAD + t * rows - 8 * jj - 8, 8)
            window = mixed[pl.ds(start, rows + 8), :]
            weights = taps[section, jj]
            for c in range(8):
                total = total + weights[c:c + 1, :] * window[8 - c:8 - c + rows, :]
            return total

        filtered = lax.fori_loop(0, taps.shape[1], tap_block, jnp.zeros((rows, LANES), F32))
        gat[span(t), lanes(ctx)] = (query * filtered).astype(BF)
        g_copy(0, t).start()
        g_copy(1, t).start()

    def emit(s, t):
        g_copy(0, t, False).wait_recv()
        g_copy(2, t).start()

    def dot(s, t):
        section = plan[s]
        g_copy(1, t, False).wait_recv()
        g_copy(2, t, False).wait_recv()
        product = lax.dot_general(
            gat[span(t), :], w_out[section], (((1,), (1,)), ((), ())), preferred_element_type=F32
        )

        @pl.when(outer)
        def _():
            r_send[t] = product.astype(BF)
            r_copy(t).start()

        @pl.when(inner)
        def _():
            acc[t] = product

    def meet(s, t):
        @pl.when(inner)
        def _():
            r_copy(t).wait_recv()
            r_send[t] = (acc[t] + r_recv[t].astype(F32)).astype(BF)

        @pl.when(gives(s))
        def _():
            c_copy(s % 2, t).start()

    def update(s, t):
        @pl.when(takes(s))
        def _():
            parity = s % 2
            c_copy(parity, t).wait_recv()
            total = r_send[t].astype(F32) + c_recv[parity, t].astype(F32)
            h[span(t), :] = (h[span(t), :].astype(F32) + total).astype(BF)

        @pl.when(returns(s))
        def _():
            b_copy(t).start()

    def out_copy(t):
        there = span(t % each_block)
        return remote(h.at[span(t), :], out.at[there, :], o_s.at[t], o_r.at[t % each_block], {"ctx": t // each_block})

    def keep_out(t):
        there = span(t % each_block)
        return pltpu.make_async_copy(h.at[span(t), :], out.at[there, :], o_s.at[t])

    def leave(s, t):
        @pl.when((s + 1 == STEPS) & corner)
        def _():
            @pl.when(outer)
            def _():
                b_copy(t).wait_recv()

            @pl.when(t // each_block != ctx)
            def _():
                out_copy(t).start()

            @pl.when(t // each_block == ctx)
            def _():
                keep_out(t).start()

    stages = (
        (ARRIVE, leave), (UPDATE, update), (MEET, meet), (DOT, dot), (EMIT, emit), (MIX, mix), (CROSS, cross), (0, enter),
    )

    def tick(u):
        @pl.when(u < each_block)
        def _():
            relay(u)

        for lag, body in stages:
            @pl.when((u >= lag) & (u < items + lag))
            def _():
                n = u - lag
                body(n // CHUNKS, n % CHUNKS)

    mixed[pl.ds(0, PAD), :] = jnp.zeros((PAD, LANES), F32)
    ss_own[...] = jnp.zeros(ss_own.shape, F32)
    each(each_block, first)
    each(items + ARRIVE, tick)

    def finish(t):
        settle(STEPS - 1, t)

        @pl.when(corner & (t // each_block != ctx))
        def _():
            out_copy(t).wait_send()

        @pl.when(corner & (t // each_block == ctx))
        def _():
            keep_out(t).wait()

    each(CHUNKS, finish)

    def received(j):
        relay_settle(j)

        @pl.when(jnp.logical_not(corner))
        def _():
            out_copy(j).wait_recv()

    each(each_block, received)


def wave(stream, in_weights, out_weights, short_taps, medium_taps, plan):
    n_ctx = lax.axis_size("ctx")
    n_chan = lax.axis_size("chan")
    ctx = lax.axis_index("ctx")
    features, channels = in_weights.shape[1], in_weights.shape[3]
    tokens = stream.shape[0] * n_ctx
    rows = tokens // CHUNKS
    each_block = CHUNKS // n_ctx
    block = 3 * LANES
    reach = medium_taps.shape[0]
    w_in = in_weights.transpose(0, 2, 1, 3)
    taps = jnp.stack([section_taps(section, short_taps, medium_taps) for section in range(2)])
    taps = lax.dynamic_slice_in_dim(taps, ctx * LANES, LANES, 2).astype(F32)
    taps = taps.reshape(2, reach // 8, 8, LANES)
    vmem = pl.BlockSpec(memory_space=pltpu.VMEM)
    dma = pltpu.SemaphoreType.DMA
    scratch = [
        pltpu.VMEM((tokens, features), BF),
        pltpu.VMEM((n_chan, stream.shape[0], features), BF),
        pltpu.VMEM((2, CHUNKS, rows, block), BF),
        pltpu.VMEM((2, CHUNKS, rows, block), BF),
        pltpu.VMEM((CHUNKS, rows, block), BF),
        pltpu.VMEM((CHUNKS, rows, block), BF),
        pltpu.VMEM((CHUNKS, rows, block), F32),
        pltpu.VMEM((CHUNKS, 8, LANES), F32),
        pltpu.VMEM((3, CHUNKS, 8, LANES), F32),
        pltpu.VMEM((PAD + tokens, LANES), F32),
        pltpu.VMEM((tokens, channels), BF),
        pltpu.VMEM((CHUNKS, rows, features), F32),
        pltpu.VMEM((CHUNKS, rows, features), BF),
        pltpu.VMEM((CHUNKS, rows, features), BF),
        pltpu.VMEM((2, CHUNKS, rows, features), BF),
        dma((n_chan, each_block)), dma((n_chan, each_block)), dma((n_chan, each_block)),
        dma((n_chan, each_block)), dma((CHUNKS,)),
        dma((3, CHUNKS)), dma((3, CHUNKS)),
        dma((2, CHUNKS)), dma((2, CHUNKS)),
        dma((CHUNKS,)), dma((CHUNKS,)),
        dma((3, CHUNKS)), dma((3, CHUNKS)),
        dma((CHUNKS,)), dma((CHUNKS,)),
        dma((2, CHUNKS)), dma((2, CHUNKS)),
        dma((CHUNKS,)), dma((CHUNKS,)),
        dma((CHUNKS,)), dma((each_block,)),
    ]
    sizes = (tokens, rows, block, features * n_ctx)
    return pl.pallas_call(
        partial(wave_kernel, sizes),
        out_shape=jax.ShapeDtypeStruct(stream.shape, stream.dtype),
        in_specs=[pl.BlockSpec(memory_space=pltpu.SMEM)] + [vmem] * 4,
        out_specs=vmem,
        scratch_shapes=scratch,
        compiler_params=pltpu.CompilerParams(
            collective_id=0, has_side_effects=True, vmem_limit_bytes=60 * 1024 * 1024
        ),
    )(plan, stream, w_in, out_weights, taps)


def fits(mesh, stream, in_weights, medium_taps):
    n_ctx, n_chan = mesh.shape["ctx"], mesh.shape["chan"]
    tokens = stream.shape[0] // mesh.shape["groups"]
    channels = in_weights.shape[3] // n_chan
    return (
        n_ctx == 4 and n_chan == 4 and channels == n_ctx * LANES
        and stream.shape[1] // n_chan == in_weights.shape[1] // n_ctx
        and tokens == 768 and medium_taps.shape[0] == PAD
    )


def solution(mesh):
    def run(stream, in_weights, out_weights, short_taps, medium_taps, plan):
        body = wave if fits(mesh, stream, in_weights, medium_taps) else shards
        return jax.shard_map(
            body,
            mesh=mesh,
            in_specs=(
                P(("groups", "ctx"), "chan"),
                P(None, "ctx", None, "chan"),
                P(None, "ctx", "chan"),
                P(None, "chan"),
                P(None, "chan"),
                P(),
            ),
            out_specs=P(("groups", "ctx"), "chan"),
            check_vma=False,
        )(stream, in_weights, out_weights, short_taps, medium_taps, plan)

    return run
```

```python
from functools import partial

import jax
import jax.numpy as jnp
from jax import lax
from jax.experimental import pallas as pl
from jax.experimental.pallas import tpu as pltpu
from jax.sharding import PartitionSpec as P

STEPS = 4


def passed_along(value, axis, steps):
    count = lax.axis_size(axis)
    leading, last = (max(0, -steps), min(count, count - steps))
    return lax.ppermute(value, axis, [(source, source + steps) for source in range(leading, last)])


def section_taps(section, short_taps, medium_taps):
    reach = medium_taps.shape[0]
    channels = short_taps.shape[1]
    padding = jnp.zeros((reach - short_taps.shape[0], channels), short_taps.dtype)
    short_full = jnp.concatenate([short_taps, padding], 0)
    group_size = channels // medium_taps.shape[1]
    medium_full = jnp.broadcast_to(
        medium_taps[:, :, None], (reach, medium_taps.shape[1], group_size)
    ).reshape(reach, channels)
    return jnp.where(section == 0, short_full, medium_full)


def causal_filter(extended, filter_taps):
    filtered = lax.conv_general_dilated(
        extended[None],
        filter_taps[::-1][:, None, :],
        (1,),
        "VALID",
        dimension_numbers=("NWC", "WIO", "NWC"),
        feature_group_count=filter_taps.shape[1],
        preferred_element_type=jnp.float32,
    )
    return filtered[0]


def filter_gate(projected, section, short_taps, medium_taps):
    query_bf = projected[:, 0].astype(jnp.bfloat16)
    mixed_bf = (projected[:, 1] * projected[:, 2]).astype(jnp.bfloat16)
    reach = medium_taps.shape[0]
    earlier = passed_along(mixed_bf[-reach:], "ctx", 1)
    extended = jnp.concatenate([earlier[1:], mixed_bf], 0)
    filtered = causal_filter(extended, section_taps(section, short_taps, medium_taps))
    return (query_bf.astype(jnp.float32) * filtered).astype(jnp.bfloat16)


def expand_rows(hidden):
    return lax.all_gather(hidden, "chan", axis=1, tiled=True)


def combine(hidden, partial_sum):
    update = lax.psum_scatter(
        partial_sum.astype(jnp.bfloat16), "chan", scatter_dimension=1, tiled=True
    ).astype(jnp.float32)
    return (hidden.astype(jnp.float32) + update).astype(jnp.bfloat16)


def advance(hidden, section, project, emit, short_taps, medium_taps):
    full_rows = expand_rows(hidden)
    widened = full_rows.astype(jnp.float32)
    row_scale = lax.rsqrt(jnp.mean(widened * widened, axis=1, keepdims=True) + 1e-05)
    projected, kept_in = project(full_rows, section)
    projected = projected.reshape(full_rows.shape[0], 3, -1) * row_scale[:, :, None]
    gated_bf = filter_gate(projected, section, short_taps, medium_taps)
    partial_sum, kept_out = emit(gated_bf, section)
    return (combine(hidden, partial_sum), kept_in, kept_out)


def stored_project(weights_in, full_rows, section):
    chosen = lax.dynamic_index_in_dim(weights_in, section, 0, keepdims=False)
    projected = jnp.dot(
        full_rows, chosen.reshape(chosen.shape[0], -1), preferred_element_type=jnp.float32
    )
    return (projected, weights_in)


def stored_emit(weights_out, gated_bf, section):
    chosen = lax.dynamic_index_in_dim(weights_out, section, 0, keepdims=False)
    product = lax.dot_general(
        gated_bf, chosen, (((1,), (1,)), ((), ())), preferred_element_type=jnp.float32
    )
    return (product, weights_out)


def shards(stream, in_weights, out_weights, short_taps, medium_taps, plan):
    hidden = stream
    weights_in, weights_out = (
        lax.all_gather(in_weights, "ctx", axis=1, tiled=True),
        lax.all_gather(out_weights, "ctx", axis=1, tiled=True),
    )
    first_step = 0
    for step_index in range(first_step, STEPS):
        hidden, weights_in, weights_out = advance(
            hidden,
            plan[step_index],
            partial(stored_project, weights_in),
            partial(stored_emit, weights_out),
            short_taps,
            medium_taps,
        )
    return hidden


CHUNKS = 12
CROSS, MIX, DOT, MEET, UPDATE, ARRIVE = 1, 3, 5, 7, 9, 12
PAD = 128
LANES = 128
BF = jnp.bfloat16
F32 = jnp.float32


def wave_kernel(
    sizes, plan, stream, w_in_hbm, w_out_hbm, short_taps, medium_taps, out,
    h, w_in, w_out, taps, land, p_send, p_recv, x_send, x_recv, own, ss_own, ss_recv, mixed, gat, acc, r_send, r_recv, c_recv,
    i_r, up_s, down_s, m_s, m_r, ss_s, ss_r, p_s, p_r, x_s, x_r, g_s, g_r, r_s, r_r, c_s, c_r, b_s, b_r, o_s, o_r, w_s,
):
    tokens, rows, block, width = sizes
    ctx, chan = lax.axis_index("ctx"), lax.axis_index("chan")
    n_ctx, n_chan = 4, 4
    side, core = ctx // 2, ctx % 2
    partner = {"ctx": side * 2 + (1 - core)}
    across = {"ctx": (1 - side) * 2 + core}
    diagonal = {"ctx": (1 - side) * 2 + (1 - core)}
    relations = (partner, across, diagonal)
    last = n_chan - 1
    outer = (chan == 0) | (chan == last)
    inner = jnp.logical_not(outer)
    near = {"chan": chan + 1 - 2 * (chan % 2)}
    mid = {"chan": jnp.where(outer, near["chan"], last - chan)}
    above = {"chan": jnp.minimum(chan + 1, last)}
    below = {"chan": jnp.maximum(chan - 1, 0)}
    corner = ctx == chan
    items = STEPS * CHUNKS
    each_block = CHUNKS // n_ctx

    def remote(source, target, send, recv, device):
        return pltpu.make_async_remote_copy(
            src_ref=source, dst_ref=target, send_sem=send, recv_sem=recv,
            device_id=device, device_id_type=pl.DeviceIdType.MESH,
        )

    def span(t):
        return pl.ds(pl.multiple_of(t * rows, rows), rows)

    def lanes(index):
        return pl.ds(pl.multiple_of(index * LANES, LANES), LANES)

    def each(count, body):
        def wrapped(t, carry):
            body(t)
            return carry
        lax.fori_loop(0, count, wrapped, 0)

    barrier = pltpu.get_barrier_semaphore()
    for di in range(n_ctx):
        for dk in range(n_chan):
            if di or dk:
                pl.semaphore_signal(
                    barrier, inc=1,
                    device_id={"ctx": (ctx + di) % n_ctx, "chan": (chan + dk) % n_chan},
                    device_id_type=pl.DeviceIdType.MESH,
                )
    in_load = pltpu.make_async_copy(w_in_hbm, w_in, w_s.at[0])
    out_load = pltpu.make_async_copy(w_out_hbm, w_out, w_s.at[1])
    pl.semaphore_wait(barrier, n_ctx * n_chan - 1)

    def hop_copy(source, q, j, upward):
        sems, device = (up_s, above) if upward else (down_s, below)
        return remote(source, land.at[q, span(j), :], sems.at[q, j], i_r.at[q, j], device)

    def spread_copy(source, q, j):
        chunk = ctx * each_block + j
        return remote(source, h.at[span(chunk), :], m_s.at[q, j], m_r.at[chunk], {"ctx": q})

    def keep_copy(source, j):
        chunk = ctx * each_block + j
        return pltpu.make_async_copy(source, h.at[span(chunk), :], m_r.at[chunk])

    def spread(source, q, j):
        @pl.when(q != ctx)
        def _():
            spread_copy(source, q, j).start()

        @pl.when(q == ctx)
        def _():
            keep_copy(source, j).start()

    def first(j):
        source = stream.at[span(j), :]

        @pl.when(chan < last)
        def _():
            hop_copy(source, chan, j, True).start()

        @pl.when(chan > 0)
        def _():
            hop_copy(source, chan, j, False).start()

        spread(source, chan, j)

    def relay(j):
        for distance in range(1, n_chan):
            @pl.when(chan >= distance)
            def _():
                q = chan - distance
                source = land.at[q, span(j), :]
                hop_copy(source, q, j, True).wait_recv()

                @pl.when(chan < last)
                def _():
                    hop_copy(source, q, j, True).start()

                spread(source, q, j)

            @pl.when(chan + distance <= last)
            def _():
                q = chan + distance
                source = land.at[q, span(j), :]
                hop_copy(source, q, j, False).wait_recv()

                @pl.when(chan > 0)
                def _():
                    hop_copy(source, q, j, False).start()

                spread(source, q, j)

    def relay_settle(j):
        for q in range(n_chan):
            source = land.at[q, span(j), :]

            @pl.when((q <= chan) & (chan < last))
            def _():
                hop_copy(source, q, j, True).wait_send()

            @pl.when((q >= chan) & (chan > 0))
            def _():
                hop_copy(source, q, j, False).wait_send()

            @pl.when(q != ctx)
            def _():
                spread_copy(source, q, j).wait_send()

    def first_arrive(t):
        @pl.when(t // each_block == ctx)
        def _():
            pltpu.make_async_copy(stream.at[span(0), :], h.at[span(t), :], m_r.at[t]).wait()

        @pl.when(t // each_block != ctx)
        def _():
            remote(stream.at[span(0), :], h.at[span(t), :], m_s.at[0, 0], m_r.at[t], partner).wait_recv()

    def ss_copy(rel, t):
        return remote(ss_own.at[t], ss_recv.at[rel, t], ss_s.at[rel, t], ss_r.at[rel, t], relations[rel])

    def p_copy(slot, t):
        return remote(p_send.at[slot, t], p_recv.at[slot, t], p_s.at[slot, t], p_r.at[slot, t], partner)

    def x_copy(t):
        return remote(x_send.at[t], x_recv.at[t], x_s.at[t], x_r.at[t], across)

    def g_copy(rel, t, sending=True):
        ref = gat.at[span(t), lanes(ctx if sending else relations[rel]["ctx"])]
        return remote(ref, ref, g_s.at[rel, t], g_r.at[rel, t], relations[rel])

    def r_copy(t):
        return remote(r_send.at[t], r_recv.at[t], r_s.at[t], r_r.at[t], near)

    def c_copy(parity, t):
        return remote(r_send.at[t], c_recv.at[parity, t], c_s.at[parity, t], c_r.at[parity, t], mid)

    def b_copy(t):
        ref = h.at[span(t), :]
        return remote(ref, ref, b_s.at[t], b_r.at[t], near)

    home = side == chan // 2

    def gives(s):
        return inner & ((s + 1 < STEPS) | jnp.logical_not(home))

    def takes(s):
        return inner & ((s + 1 < STEPS) | home)

    def returns(s):
        return inner & ((s + 1 < STEPS) | (ctx == near["chan"]))

    def awaits(s):
        return outer & ((s + 1 < STEPS) | corner)

    def settle(s, t):
        for slot in range(2):
            p_copy(slot, t).wait_send()
        for rel in range(3):
            ss_copy(rel, t).wait_send()
        x_copy(t).wait_send()
        for kind in range(3):
            g_copy(kind, t).wait_send()

        @pl.when(outer)
        def _():
            r_copy(t).wait_send()

        @pl.when(gives(s))
        def _():
            c_copy(s % 2, t).wait_send()

        @pl.when(returns(s))
        def _():
            b_copy(t).wait_send()

    def project(section, t, index):
        columns = lanes(index)
        weights = jnp.concatenate([w_in[section, j, :, columns] for j in range(3)], 1)
        return jnp.dot(h[span(t), :], weights, preferred_element_type=F32)

    def enter(s, t):
        section = plan[s]

        @pl.when(s > 0)
        def _():
            settle(s - 1, t)

            @pl.when(outer)
            def _():
                b_copy(t).wait_recv()

        @pl.when(s == 0)
        def _():
            first_arrive(t)

        p_send[0, t] = project(section, t, diagonal["ctx"]).astype(BF)
        p_copy(0, t).start()
        p_send[1, t] = project(section, t, partner["ctx"]).astype(BF)
        p_copy(1, t).start()
        wide = h[span(t), :].astype(F32)
        squares = (wide * wide).astype(BF)
        ss_own[t, :, pl.ds(0, rows)] = lax.dot_general(
            jnp.ones((8, squares.shape[1]), BF), squares, (((1,), (1,)), ((), ())), preferred_element_type=F32
        )
        for rel in range(3):
            ss_copy(rel, t).start()

    def cross(s, t):
        section = plan[s]
        passing = project(section, t, across["ctx"])
        p_copy(0, t).wait_recv()
        x_send[t] = (passing + p_recv[0, t].astype(F32)).astype(BF)
        x_copy(t).start()
        own[t] = project(section, t, ctx)

    def mix(s, t):
        section = plan[s]
        for rel in range(3):
            ss_copy(rel, t).wait_recv()
        p_copy(1, t).wait_recv()
        x_copy(t).wait_recv()
        total = ss_own[t] + ss_recv[0, t] + ss_recv[1, t] + ss_recv[2, t]
        scale = lax.rsqrt(total * (1.0 / width) + 1e-05)
        scale = jnp.transpose(scale)[:rows, :1]
        parts = (own[t] + p_recv[1, t].astype(F32) + x_recv[t].astype(F32)) * scale
        query = parts[:, :LANES].astype(BF).astype(F32)
        product = parts[:, LANES:2 * LANES] * parts[:, 2 * LANES:]
        base = PAD + t * rows
        before = mixed[0, pl.ds(pl.multiple_of(base - 8, 8), 8), :]
        window = jnp.concatenate([before, product.astype(BF).astype(F32)], 0)
        for c in range(8):
            mixed[c, pl.ds(pl.multiple_of(base, rows), rows), :] = window[8 - c:8 - c + rows, :]

        def tap_block(jj, total):
            here = pl.ds(pl.multiple_of(base - 8 * jj, 8), rows)
            weights = taps[section, jj]
            for c in range(8):
                total = total + weights[c:c + 1, :] * mixed[c, here, :]
            return total

        filtered = lax.fori_loop(0, taps.shape[1], tap_block, jnp.zeros((rows, LANES), F32))
        gat[span(t), lanes(ctx)] = (query * filtered).astype(BF)
        for rel in (2, 1, 0):
            g_copy(rel, t).start()

    def dot(s, t):
        section = plan[s]
        for rel in range(3):
            g_copy(rel, t, False).wait_recv()
        product = lax.dot_general(
            gat[span(t), :], w_out[section], (((1,), (1,)), ((), ())), preferred_element_type=F32
        )

        @pl.when(outer)
        def _():
            r_send[t] = product.astype(BF)
            r_copy(t).start()

        @pl.when(inner)
        def _():
            acc[t] = product

    def meet(s, t):
        @pl.when(inner)
        def _():
            r_copy(t).wait_recv()
            r_send[t] = (acc[t] + r_recv[t].astype(F32)).astype(BF)

        @pl.when(gives(s))
        def _():
            c_copy(s % 2, t).start()

    def update(s, t):
        @pl.when(takes(s))
        def _():
            parity = s % 2
            c_copy(parity, t).wait_recv()
            total = r_send[t].astype(F32) + c_recv[parity, t].astype(F32)
            h[span(t), :] = (h[span(t), :].astype(F32) + total).astype(BF)

        @pl.when(returns(s))
        def _():
            b_copy(t).start()

    def out_copy(t):
        there = span(t % each_block)
        return remote(h.at[span(t), :], out.at[there, :], o_s.at[t], o_r.at[t % each_block], {"ctx": t // each_block})

    def keep_out(t):
        there = span(t % each_block)
        return pltpu.make_async_copy(h.at[span(t), :], out.at[there, :], o_s.at[t])

    def leave(s, t):
        @pl.when((s + 1 == STEPS) & corner)
        def _():
            @pl.when(outer)
            def _():
                b_copy(t).wait_recv()

            @pl.when(t // each_block != ctx)
            def _():
                out_copy(t).start()

            @pl.when(t // each_block == ctx)
            def _():
                keep_out(t).start()

    stages = (
        (ARRIVE, leave), (UPDATE, update), (MEET, meet), (DOT, dot), (MIX, mix), (CROSS, cross), (0, enter),
    )

    def tick(u):
        @pl.when(u < each_block)
        def _():
            relay(u)

        for lag, body in stages:
            @pl.when((u >= lag) & (u < items + lag))
            def _():
                n = u - lag
                body(n // CHUNKS, n % CHUNKS)

    each(each_block, first)
    in_load.start()
    out_load.start()
    for c in range(8):
        mixed[c, pl.ds(0, PAD), :] = jnp.zeros((PAD, LANES), F32)
    ss_own[...] = jnp.zeros(ss_own.shape, F32)
    groups, reach = medium_taps.shape
    share = LANES // (groups // n_ctx)
    row = lax.broadcasted_iota(jnp.int32, (groups, LANES), 0)
    lane = lax.broadcasted_iota(jnp.int32, (groups, LANES), 1)
    chosen = jnp.where(row == ctx * (groups // n_ctx) + lane // share, 1.0, 0.0).astype(BF)
    spread_taps = lax.dot_general(
        medium_taps[...], chosen, (((0,), (0,)), ((), ())), preferred_element_type=F32
    )
    taps[1] = spread_taps.reshape(reach // 8, 8, LANES)
    taps[0] = jnp.zeros((reach // 8, 8, LANES), F32)
    count = short_taps.shape[0]
    taps[0, 0, pl.ds(0, count), :] = short_taps[:, lanes(ctx)].astype(F32)
    in_load.wait()
    out_load.wait()
    each(items + ARRIVE, tick)

    def finish(t):
        settle(STEPS - 1, t)

        @pl.when(corner & (t // each_block != ctx))
        def _():
            out_copy(t).wait_send()

        @pl.when(corner & (t // each_block == ctx))
        def _():
            keep_out(t).wait()

    each(CHUNKS, finish)

    def received(j):
        relay_settle(j)

        @pl.when(jnp.logical_not(corner))
        def _():
            out_copy(j).wait_recv()

    each(each_block, received)


def wave(stream, in_weights, out_weights, short_taps, medium_taps, plan):
    n_ctx = lax.axis_size("ctx")
    n_chan = lax.axis_size("chan")
    features, channels = in_weights.shape[1], in_weights.shape[3]
    tokens = stream.shape[0] * n_ctx
    rows = tokens // CHUNKS
    each_block = CHUNKS // n_ctx
    block = 3 * LANES
    reach = medium_taps.shape[0]
    w_in = in_weights.transpose(0, 2, 1, 3)
    vmem = pl.BlockSpec(memory_space=pltpu.VMEM)
    anywhere = pl.BlockSpec(memory_space=pl.ANY)
    dma = pltpu.SemaphoreType.DMA
    scratch = [
        pltpu.VMEM((tokens, features), BF),
        pltpu.VMEM(w_in.shape, BF),
        pltpu.VMEM(out_weights.shape, BF),
        pltpu.VMEM((2, reach // 8, 8, LANES), F32),
        pltpu.VMEM((n_chan, stream.shape[0], features), BF),
        pltpu.VMEM((2, CHUNKS, rows, block), BF),
        pltpu.VMEM((2, CHUNKS, rows, block), BF),
        pltpu.VMEM((CHUNKS, rows, block), BF),
        pltpu.VMEM((CHUNKS, rows, block), BF),
        pltpu.VMEM((CHUNKS, rows, block), F32),
        pltpu.VMEM((CHUNKS, 8, LANES), F32),
        pltpu.VMEM((3, CHUNKS, 8, LANES), F32),
        pltpu.VMEM((8, PAD + tokens, LANES), F32),
        pltpu.VMEM((tokens, channels), BF),
        pltpu.VMEM((CHUNKS, rows, features), F32),
        pltpu.VMEM((CHUNKS, rows, features), BF),
        pltpu.VMEM((CHUNKS, rows, features), BF),
        pltpu.VMEM((2, CHUNKS, rows, features), BF),
        dma((n_chan, each_block)), dma((n_chan, each_block)), dma((n_chan, each_block)),
        dma((n_chan, each_block)), dma((CHUNKS,)),
        dma((3, CHUNKS)), dma((3, CHUNKS)),
        dma((2, CHUNKS)), dma((2, CHUNKS)),
        dma((CHUNKS,)), dma((CHUNKS,)),
        dma((3, CHUNKS)), dma((3, CHUNKS)),
        dma((CHUNKS,)), dma((CHUNKS,)),
        dma((2, CHUNKS)), dma((2, CHUNKS)),
        dma((CHUNKS,)), dma((CHUNKS,)),
        dma((CHUNKS,)), dma((each_block,)), dma((2,)),
    ]
    sizes = (tokens, rows, block, features * n_ctx)
    return pl.pallas_call(
        partial(wave_kernel, sizes),
        out_shape=jax.ShapeDtypeStruct(stream.shape, stream.dtype),
        in_specs=[pl.BlockSpec(memory_space=pltpu.SMEM), vmem, anywhere, anywhere, vmem, vmem],
        out_specs=vmem,
        scratch_shapes=scratch,
        compiler_params=pltpu.CompilerParams(
            collective_id=0, has_side_effects=True, vmem_limit_bytes=60 * 1024 * 1024
        ),
    )(plan, stream, w_in, out_weights, short_taps, medium_taps.T)


def fits(mesh, stream, in_weights, medium_taps):
    n_ctx, n_chan = mesh.shape["ctx"], mesh.shape["chan"]
    tokens = stream.shape[0] // mesh.shape["groups"]
    channels = in_weights.shape[3] // n_chan
    return (
        n_ctx == 4 and n_chan == 4 and channels == n_ctx * LANES
        and stream.shape[1] // n_chan == in_weights.shape[1] // n_ctx
        and tokens == 768 and medium_taps.shape[0] == PAD
    )


def solution(mesh):
    def run(stream, in_weights, out_weights, short_taps, medium_taps, plan):
        body = wave if fits(mesh, stream, in_weights, medium_taps) else shards
        return jax.shard_map(
            body,
            mesh=mesh,
            in_specs=(
                P(("groups", "ctx"), "chan"),
                P(None, "ctx", None, "chan"),
                P(None, "ctx", "chan"),
                P(None, "chan"),
                P(None, "chan"),
                P(),
            ),
            out_specs=P(("groups", "ctx"), "chan"),
            check_vma=False,
        )(stream, in_weights, out_weights, short_taps, medium_taps, plan)

    return run
```

```python
from functools import partial

import jax
import jax.numpy as jnp
from jax import lax
from jax.experimental import pallas as pl
from jax.experimental.pallas import tpu as pltpu
from jax.sharding import PartitionSpec as P

STEPS = 4


def passed_along(value, axis, steps):
    count = lax.axis_size(axis)
    leading, last = (max(0, -steps), min(count, count - steps))
    return lax.ppermute(value, axis, [(source, source + steps) for source in range(leading, last)])


def section_taps(section, short_taps, medium_taps):
    reach = medium_taps.shape[0]
    channels = short_taps.shape[1]
    padding = jnp.zeros((reach - short_taps.shape[0], channels), short_taps.dtype)
    short_full = jnp.concatenate([short_taps, padding], 0)
    group_size = channels // medium_taps.shape[1]
    medium_full = jnp.broadcast_to(
        medium_taps[:, :, None], (reach, medium_taps.shape[1], group_size)
    ).reshape(reach, channels)
    return jnp.where(section == 0, short_full, medium_full)


def causal_filter(extended, filter_taps):
    filtered = lax.conv_general_dilated(
        extended[None],
        filter_taps[::-1][:, None, :],
        (1,),
        "VALID",
        dimension_numbers=("NWC", "WIO", "NWC"),
        feature_group_count=filter_taps.shape[1],
        preferred_element_type=jnp.float32,
    )
    return filtered[0]


def filter_gate(projected, section, short_taps, medium_taps):
    query_bf = projected[:, 0].astype(jnp.bfloat16)
    mixed_bf = (projected[:, 1] * projected[:, 2]).astype(jnp.bfloat16)
    reach = medium_taps.shape[0]
    earlier = passed_along(mixed_bf[-reach:], "ctx", 1)
    extended = jnp.concatenate([earlier[1:], mixed_bf], 0)
    filtered = causal_filter(extended, section_taps(section, short_taps, medium_taps))
    return (query_bf.astype(jnp.float32) * filtered).astype(jnp.bfloat16)


def expand_rows(hidden):
    return lax.all_gather(hidden, "chan", axis=1, tiled=True)


def combine(hidden, partial_sum):
    update = lax.psum_scatter(
        partial_sum.astype(jnp.bfloat16), "chan", scatter_dimension=1, tiled=True
    ).astype(jnp.float32)
    return (hidden.astype(jnp.float32) + update).astype(jnp.bfloat16)


def advance(hidden, section, project, emit, short_taps, medium_taps):
    full_rows = expand_rows(hidden)
    widened = full_rows.astype(jnp.float32)
    row_scale = lax.rsqrt(jnp.mean(widened * widened, axis=1, keepdims=True) + 1e-05)
    projected, kept_in = project(full_rows, section)
    projected = projected.reshape(full_rows.shape[0], 3, -1) * row_scale[:, :, None]
    gated_bf = filter_gate(projected, section, short_taps, medium_taps)
    partial_sum, kept_out = emit(gated_bf, section)
    return (combine(hidden, partial_sum), kept_in, kept_out)


def stored_project(weights_in, full_rows, section):
    chosen = lax.dynamic_index_in_dim(weights_in, section, 0, keepdims=False)
    projected = jnp.dot(
        full_rows, chosen.reshape(chosen.shape[0], -1), preferred_element_type=jnp.float32
    )
    return (projected, weights_in)


def stored_emit(weights_out, gated_bf, section):
    chosen = lax.dynamic_index_in_dim(weights_out, section, 0, keepdims=False)
    product = lax.dot_general(
        gated_bf, chosen, (((1,), (1,)), ((), ())), preferred_element_type=jnp.float32
    )
    return (product, weights_out)


def shards(stream, in_weights, out_weights, short_taps, medium_taps, plan):
    hidden = stream
    weights_in, weights_out = (
        lax.all_gather(in_weights, "ctx", axis=1, tiled=True),
        lax.all_gather(out_weights, "ctx", axis=1, tiled=True),
    )
    first_step = 0
    for step_index in range(first_step, STEPS):
        hidden, weights_in, weights_out = advance(
            hidden,
            plan[step_index],
            partial(stored_project, weights_in),
            partial(stored_emit, weights_out),
            short_taps,
            medium_taps,
        )
    return hidden


CHUNKS = 12
CROSS, MIX, DOT, MEET, UPDATE = 1, 3, 5, 7, 9
PAD = 128
LANES = 128
BF = jnp.bfloat16
F32 = jnp.float32


def wave_kernel(
    sizes, plan, stream_hbm, w_in_hbm, w_out_hbm, short_taps, medium_taps, out,
    h, w_in, w_out, taps, land, p_send, p_recv, x_send, x_recv, own, ss_own, ss_recv, mixed, gat, acc, r_send, r_recv, c_recv,
    i_r, up_s, down_s, m_s, m_r, ss_s, ss_r, p_s, p_r, x_s, x_r, g_s, g_r, r_s, r_r, c_s, c_r, b_s, b_r, o_s, o_r, w_s,
):
    tokens, rows, block, width = sizes
    ctx, chan = lax.axis_index("ctx"), lax.axis_index("chan")
    n_ctx, n_chan = 4, 4
    side, core = ctx // 2, ctx % 2
    partner = {"ctx": side * 2 + (1 - core)}
    across = {"ctx": (1 - side) * 2 + core}
    diagonal = {"ctx": (1 - side) * 2 + (1 - core)}
    relations = (partner, across, diagonal)
    last = n_chan - 1
    outer = (chan == 0) | (chan == last)
    inner = jnp.logical_not(outer)
    near = {"chan": chan + 1 - 2 * (chan % 2)}
    mid = {"chan": jnp.where(outer, near["chan"], last - chan)}
    above = {"chan": jnp.minimum(chan + 1, last)}
    below = {"chan": jnp.maximum(chan - 1, 0)}
    corner = ctx == chan
    items = STEPS * CHUNKS
    each_block = CHUNKS // n_ctx

    def remote(source, target, send, recv, device):
        return pltpu.make_async_remote_copy(
            src_ref=source, dst_ref=target, send_sem=send, recv_sem=recv,
            device_id=device, device_id_type=pl.DeviceIdType.MESH,
        )

    def span(t):
        return pl.ds(pl.multiple_of(t * rows, rows), rows)

    def lanes(index):
        return pl.ds(pl.multiple_of(index * LANES, LANES), LANES)

    def each(count, body):
        def wrapped(t, carry):
            body(t)
            return carry
        lax.fori_loop(0, count, wrapped, 0)

    barrier = pltpu.get_barrier_semaphore()

    def greet(**device):
        pl.semaphore_signal(barrier, inc=1, device_id=device, device_id_type=pl.DeviceIdType.MESH)

    for di in range(1, n_ctx):
        greet(ctx=(ctx + di) % n_ctx, chan=chan)

    @pl.when(chan < last)
    def _():
        greet(ctx=ctx, chan=chan + 1)

    @pl.when(chan > 0)
    def _():
        greet(ctx=ctx, chan=chan - 1)

    @pl.when(outer & (ctx != chan))
    def _():
        greet(ctx=chan, chan=near["chan"])

    guests = n_ctx - 1 + jnp.where(outer, 1, 2) + jnp.where(inner & (ctx == near["chan"]), n_ctx - 1, 0)
    own_load = pltpu.make_async_copy(stream_hbm, land.at[chan], w_s.at[2])
    own_load.start()
    in_load = pltpu.make_async_copy(w_in_hbm, w_in, w_s.at[0])
    out_load = pltpu.make_async_copy(w_out_hbm, w_out, w_s.at[1])
    in_load.start()
    out_load.start()
    for c in range(8):
        mixed[c, pl.ds(0, PAD), :] = jnp.zeros((PAD, LANES), F32)
    ss_own[...] = jnp.zeros(ss_own.shape, F32)
    groups, reach = medium_taps.shape
    share = LANES // (groups // n_ctx)
    row = lax.broadcasted_iota(jnp.int32, (groups, LANES), 0)
    lane = lax.broadcasted_iota(jnp.int32, (groups, LANES), 1)
    chosen = jnp.where(row == ctx * (groups // n_ctx) + lane // share, 1.0, 0.0).astype(BF)
    spread_taps = lax.dot_general(
        medium_taps[...], chosen, (((0,), (0,)), ((), ())), preferred_element_type=F32
    )
    taps[1] = spread_taps.reshape(reach // 8, 8, LANES)
    taps[0] = jnp.zeros((reach // 8, 8, LANES), F32)
    count = short_taps.shape[0]
    taps[0, 0, pl.ds(0, count), :] = short_taps[:, lanes(ctx)].astype(F32)
    pl.semaphore_wait(barrier, guests)
    own_load.wait()

    def hop_copy(source, q, j, upward):
        sems, device = (up_s, above) if upward else (down_s, below)
        return remote(source, land.at[q, span(j), :], sems.at[q, j], i_r.at[q, j], device)

    def spread_copy(source, q, j):
        chunk = ctx * each_block + j
        return remote(source, h.at[span(chunk), :], m_s.at[q, j], m_r.at[chunk], {"ctx": q})

    def keep_copy(source, j):
        chunk = ctx * each_block + j
        return pltpu.make_async_copy(source, h.at[span(chunk), :], m_r.at[chunk])

    def spread(source, q, j):
        @pl.when(q != ctx)
        def _():
            spread_copy(source, q, j).start()

        @pl.when(q == ctx)
        def _():
            keep_copy(source, j).start()

    def first(j):
        source = land.at[chan, span(j), :]

        @pl.when(chan < last)
        def _():
            hop_copy(source, chan, j, True).start()

        @pl.when(chan > 0)
        def _():
            hop_copy(source, chan, j, False).start()

        spread(source, chan, j)

    def relay(q, j, upward):
        source = land.at[q, span(j), :]
        hop_copy(source, q, j, upward).wait_recv()

        @pl.when((chan < last) if upward else (chan > 0))
        def _():
            hop_copy(source, q, j, upward).start()

        spread(source, q, j)

    def relay_round(r):
        for distance in range(last, 0, -1):
            j = r - distance
            present = (j >= 0) & (j < each_block)

            @pl.when(present & (chan >= distance))
            def _():
                relay(chan - distance, j, True)

            @pl.when(present & (chan + distance <= last))
            def _():
                relay(chan + distance, j, False)

        @pl.when(r < each_block)
        def _():
            first(r)

    def relay_settle(j):
        for q in range(n_chan):
            source = land.at[q, span(j), :]

            @pl.when((q <= chan) & (chan < last))
            def _():
                hop_copy(source, q, j, True).wait_send()

            @pl.when((q >= chan) & (chan > 0))
            def _():
                hop_copy(source, q, j, False).wait_send()

            @pl.when(q != ctx)
            def _():
                spread_copy(source, q, j).wait_send()

    def first_arrive(t):
        @pl.when(t // each_block == ctx)
        def _():
            pltpu.make_async_copy(land.at[0, span(0), :], h.at[span(t), :], m_r.at[t]).wait()

        @pl.when(t // each_block != ctx)
        def _():
            remote(land.at[0, span(0), :], h.at[span(t), :], m_s.at[0, 0], m_r.at[t], partner).wait_recv()

    def ss_copy(rel, t):
        return remote(ss_own.at[t], ss_recv.at[rel, t], ss_s.at[rel, t], ss_r.at[rel, t], relations[rel])

    def p_copy(slot, t):
        return remote(p_send.at[slot, t], p_recv.at[slot, t], p_s.at[slot, t], p_r.at[slot, t], partner)

    def x_copy(t):
        return remote(x_send.at[t], x_recv.at[t], x_s.at[t], x_r.at[t], across)

    def g_copy(rel, t, sending=True):
        ref = gat.at[span(t), lanes(ctx if sending else relations[rel]["ctx"])]
        return remote(ref, ref, g_s.at[rel, t], g_r.at[rel, t], relations[rel])

    def r_copy(t):
        return remote(r_send.at[t], r_recv.at[t], r_s.at[t], r_r.at[t], near)

    def c_copy(parity, t):
        return remote(r_send.at[t], c_recv.at[parity, t], c_s.at[parity, t], c_r.at[parity, t], mid)

    def b_copy(t):
        ref = h.at[span(t), :]
        return remote(ref, ref, b_s.at[t], b_r.at[t], near)

    home = side == chan // 2

    def gives(s):
        return inner & ((s + 1 < STEPS) | jnp.logical_not(home))

    def takes(s):
        return inner & ((s + 1 < STEPS) | home)

    def returns(s):
        return inner & (s + 1 < STEPS)

    def settle(s, t):
        for slot in range(2):
            p_copy(slot, t).wait_send()
        for rel in range(3):
            ss_copy(rel, t).wait_send()
        x_copy(t).wait_send()
        for kind in range(3):
            g_copy(kind, t).wait_send()

        @pl.when(outer)
        def _():
            r_copy(t).wait_send()

        @pl.when(gives(s))
        def _():
            c_copy(s % 2, t).wait_send()

        @pl.when(returns(s))
        def _():
            b_copy(t).wait_send()

    def project(section, t, index):
        columns = lanes(index)
        weights = jnp.concatenate([w_in[section, j, :, columns] for j in range(3)], 1)
        return jnp.dot(h[span(t), :], weights, preferred_element_type=F32)

    def enter(s, t):
        section = plan[s]

        @pl.when(s > 0)
        def _():
            settle(s - 1, t)

            @pl.when(outer)
            def _():
                b_copy(t).wait_recv()

        @pl.when(s == 0)
        def _():
            first_arrive(t)

        p_send[0, t] = project(section, t, diagonal["ctx"]).astype(BF)
        p_copy(0, t).start()
        p_send[1, t] = project(section, t, partner["ctx"]).astype(BF)
        p_copy(1, t).start()
        wide = h[span(t), :].astype(F32)
        squares = (wide * wide).astype(BF)
        ss_own[t, :, pl.ds(0, rows)] = lax.dot_general(
            jnp.ones((8, squares.shape[1]), BF), squares, (((1,), (1,)), ((), ())), preferred_element_type=F32
        )
        for rel in range(3):
            ss_copy(rel, t).start()

    def cross(s, t):
        section = plan[s]
        passing = project(section, t, across["ctx"])
        p_copy(0, t).wait_recv()
        x_send[t] = (passing + p_recv[0, t].astype(F32)).astype(BF)
        x_copy(t).start()
        own[t] = project(section, t, ctx)

    def mix(s, t):
        section = plan[s]
        for rel in range(3):
            ss_copy(rel, t).wait_recv()
        p_copy(1, t).wait_recv()
        x_copy(t).wait_recv()
        total = ss_own[t] + ss_recv[0, t] + ss_recv[1, t] + ss_recv[2, t]
        scale = lax.rsqrt(total * (1.0 / width) + 1e-05)
        scale = jnp.transpose(scale)[:rows, :1]
        parts = (own[t] + p_recv[1, t].astype(F32) + x_recv[t].astype(F32)) * scale
        query = parts[:, :LANES].astype(BF).astype(F32)
        product = parts[:, LANES:2 * LANES] * parts[:, 2 * LANES:]
        base = PAD + t * rows
        before = mixed[0, pl.ds(pl.multiple_of(base - 8, 8), 8), :]
        window = jnp.concatenate([before, product.astype(BF).astype(F32)], 0)
        for c in range(8):
            mixed[c, pl.ds(pl.multiple_of(base, rows), rows), :] = window[8 - c:8 - c + rows, :]

        def tap_block(jj, total):
            here = pl.ds(pl.multiple_of(base - 8 * jj, 8), rows)
            weights = taps[section, jj]
            for c in range(8):
                total = total + weights[c:c + 1, :] * mixed[c, here, :]
            return total

        filtered = lax.fori_loop(0, taps.shape[1], tap_block, jnp.zeros((rows, LANES), F32))
        gat[span(t), lanes(ctx)] = (query * filtered).astype(BF)
        for rel in (2, 1, 0):
            g_copy(rel, t).start()

    def dot(s, t):
        section = plan[s]
        for rel in range(3):
            g_copy(rel, t, False).wait_recv()
        product = lax.dot_general(
            gat[span(t), :], w_out[section], (((1,), (1,)), ((), ())), preferred_element_type=F32
        )

        @pl.when(outer)
        def _():
            r_send[t] = product.astype(BF)
            r_copy(t).start()

        @pl.when(inner)
        def _():
            acc[t] = product

    def meet(s, t):
        @pl.when(inner)
        def _():
            r_copy(t).wait_recv()
            r_send[t] = (acc[t] + r_recv[t].astype(F32)).astype(BF)

        @pl.when(gives(s))
        def _():
            c_copy(s % 2, t).start()

    def out_copy(t):
        there = span(t % each_block)
        return remote(
            h.at[span(t), :], out.at[there, :], o_s.at[t], o_r.at[t % each_block],
            {"ctx": t // each_block, "chan": ctx},
        )

    def keep_out(t):
        there = span(t % each_block)
        return pltpu.make_async_copy(h.at[span(t), :], out.at[there, :], o_s.at[t])

    def stays(t):
        return corner & (t // each_block == ctx)

    def update(s, t):
        @pl.when(takes(s))
        def _():
            parity = s % 2
            c_copy(parity, t).wait_recv()
            total = r_send[t].astype(F32) + c_recv[parity, t].astype(F32)
            h[span(t), :] = (h[span(t), :].astype(F32) + total).astype(BF)

        @pl.when(returns(s))
        def _():
            b_copy(t).start()

        @pl.when((s + 1 == STEPS) & inner & home & jnp.logical_not(stays(t)))
        def _():
            out_copy(t).start()

        @pl.when((s + 1 == STEPS) & inner & home & stays(t))
        def _():
            keep_out(t).start()

    stages = (
        (UPDATE, update), (MEET, meet), (DOT, dot), (MIX, mix), (CROSS, cross), (0, enter),
    )

    def tick(u):
        for lag, body in stages:
            @pl.when((u >= lag) & (u < items + lag))
            def _():
                n = u - lag
                body(n // CHUNKS, n % CHUNKS)

        @pl.when((core == 0) & (u < each_block - 1))
        def _():
            relay_round(last + 1 + u)

        @pl.when((core == 1) & (u < 2))
        def _():
            relay_round(u)

        @pl.when((core == 1) & (u >= 2) & (u < 2 + each_block // 2 + 1))
        def _():
            for extra in range(2):
                relay_round(2 * u - 2 + extra)

    @pl.when(core == 0)
    def _():
        each(last + 1, relay_round)

    in_load.wait()
    out_load.wait()
    each(items + UPDATE, tick)

    def finish(t):
        settle(STEPS - 1, t)

        @pl.when(inner & home & jnp.logical_not(stays(t)))
        def _():
            out_copy(t).wait_send()

        @pl.when(inner & home & stays(t))
        def _():
            keep_out(t).wait()

    each(CHUNKS, finish)

    def received(j):
        relay_settle(j)

        @pl.when(jnp.logical_not(corner & inner))
        def _():
            out_copy(j).wait_recv()

    each(each_block, received)


def wave(stream, in_weights, out_weights, short_taps, medium_taps, plan):
    n_ctx = lax.axis_size("ctx")
    n_chan = lax.axis_size("chan")
    features, channels = in_weights.shape[1], in_weights.shape[3]
    tokens = stream.shape[0] * n_ctx
    rows = tokens // CHUNKS
    each_block = CHUNKS // n_ctx
    block = 3 * LANES
    reach = medium_taps.shape[0]
    w_in = in_weights.transpose(0, 2, 1, 3)
    vmem = pl.BlockSpec(memory_space=pltpu.VMEM)
    anywhere = pl.BlockSpec(memory_space=pl.ANY)
    dma = pltpu.SemaphoreType.DMA
    scratch = [
        pltpu.VMEM((tokens, features), BF),
        pltpu.VMEM(w_in.shape, BF),
        pltpu.VMEM(out_weights.shape, BF),
        pltpu.VMEM((2, reach // 8, 8, LANES), F32),
        pltpu.VMEM((n_chan, stream.shape[0], features), BF),
        pltpu.VMEM((2, CHUNKS, rows, block), BF),
        pltpu.VMEM((2, CHUNKS, rows, block), BF),
        pltpu.VMEM((CHUNKS, rows, block), BF),
        pltpu.VMEM((CHUNKS, rows, block), BF),
        pltpu.VMEM((CHUNKS, rows, block), F32),
        pltpu.VMEM((CHUNKS, 8, LANES), F32),
        pltpu.VMEM((3, CHUNKS, 8, LANES), F32),
        pltpu.VMEM((8, PAD + tokens, LANES), F32),
        pltpu.VMEM((tokens, channels), BF),
        pltpu.VMEM((CHUNKS, rows, features), F32),
        pltpu.VMEM((CHUNKS, rows, features), BF),
        pltpu.VMEM((CHUNKS, rows, features), BF),
        pltpu.VMEM((2, CHUNKS, rows, features), BF),
        dma((n_chan, each_block)), dma((n_chan, each_block)), dma((n_chan, each_block)),
        dma((n_chan, each_block)), dma((CHUNKS,)),
        dma((3, CHUNKS)), dma((3, CHUNKS)),
        dma((2, CHUNKS)), dma((2, CHUNKS)),
        dma((CHUNKS,)), dma((CHUNKS,)),
        dma((3, CHUNKS)), dma((3, CHUNKS)),
        dma((CHUNKS,)), dma((CHUNKS,)),
        dma((2, CHUNKS)), dma((2, CHUNKS)),
        dma((CHUNKS,)), dma((CHUNKS,)),
        dma((CHUNKS,)), dma((each_block,)), dma((3,)),
    ]
    sizes = (tokens, rows, block, features * n_ctx)
    return pl.pallas_call(
        partial(wave_kernel, sizes),
        out_shape=jax.ShapeDtypeStruct(stream.shape, stream.dtype),
        in_specs=[pl.BlockSpec(memory_space=pltpu.SMEM), anywhere, anywhere, anywhere, vmem, vmem],
        out_specs=anywhere,
        scratch_shapes=scratch,
        compiler_params=pltpu.CompilerParams(
            collective_id=0, has_side_effects=True, vmem_limit_bytes=60 * 1024 * 1024
        ),
    )(plan, stream, w_in, out_weights, short_taps, medium_taps.T)


def fits(mesh, stream, in_weights, medium_taps):
    n_ctx, n_chan = mesh.shape["ctx"], mesh.shape["chan"]
    tokens = stream.shape[0] // mesh.shape["groups"]
    channels = in_weights.shape[3] // n_chan
    return (
        n_ctx == 4 and n_chan == 4 and channels == n_ctx * LANES
        and stream.shape[1] // n_chan == in_weights.shape[1] // n_ctx
        and tokens == 768 and medium_taps.shape[0] == PAD
    )


def solution(mesh):
    def run(stream, in_weights, out_weights, short_taps, medium_taps, plan):
        body = wave if fits(mesh, stream, in_weights, medium_taps) else shards
        return jax.shard_map(
            body,
            mesh=mesh,
            in_specs=(
                P(("groups", "ctx"), "chan"),
                P(None, "ctx", None, "chan"),
                P(None, "ctx", "chan"),
                P(None, "chan"),
                P(None, "chan"),
                P(),
            ),
            out_specs=P(("groups", "ctx"), "chan"),
            check_vma=False,
        )(stream, in_weights, out_weights, short_taps, medium_taps, plan)

    return run
```

```python
from functools import partial

import jax
import jax.numpy as jnp
from jax import lax
from jax.experimental import pallas as pl
from jax.experimental.pallas import tpu as pltpu
from jax.sharding import PartitionSpec as P

STEPS = 4


def passed_along(value, axis, steps):
    count = lax.axis_size(axis)
    leading, last = (max(0, -steps), min(count, count - steps))
    return lax.ppermute(value, axis, [(source, source + steps) for source in range(leading, last)])


def section_taps(section, short_taps, medium_taps):
    reach = medium_taps.shape[0]
    channels = short_taps.shape[1]
    padding = jnp.zeros((reach - short_taps.shape[0], channels), short_taps.dtype)
    short_full = jnp.concatenate([short_taps, padding], 0)
    group_size = channels // medium_taps.shape[1]
    medium_full = jnp.broadcast_to(
        medium_taps[:, :, None], (reach, medium_taps.shape[1], group_size)
    ).reshape(reach, channels)
    return jnp.where(section == 0, short_full, medium_full)


def causal_filter(extended, filter_taps):
    filtered = lax.conv_general_dilated(
        extended[None],
        filter_taps[::-1][:, None, :],
        (1,),
        "VALID",
        dimension_numbers=("NWC", "WIO", "NWC"),
        feature_group_count=filter_taps.shape[1],
        preferred_element_type=jnp.float32,
    )
    return filtered[0]


def filter_gate(projected, section, short_taps, medium_taps):
    query_bf = projected[:, 0].astype(jnp.bfloat16)
    mixed_bf = (projected[:, 1] * projected[:, 2]).astype(jnp.bfloat16)
    reach = medium_taps.shape[0]
    earlier = passed_along(mixed_bf[-reach:], "ctx", 1)
    extended = jnp.concatenate([earlier[1:], mixed_bf], 0)
    filtered = causal_filter(extended, section_taps(section, short_taps, medium_taps))
    return (query_bf.astype(jnp.float32) * filtered).astype(jnp.bfloat16)


def expand_rows(hidden):
    return lax.all_gather(hidden, "chan", axis=1, tiled=True)


def combine(hidden, partial_sum):
    update = lax.psum_scatter(
        partial_sum.astype(jnp.bfloat16), "chan", scatter_dimension=1, tiled=True
    ).astype(jnp.float32)
    return (hidden.astype(jnp.float32) + update).astype(jnp.bfloat16)


def advance(hidden, section, project, emit, short_taps, medium_taps):
    full_rows = expand_rows(hidden)
    widened = full_rows.astype(jnp.float32)
    row_scale = lax.rsqrt(jnp.mean(widened * widened, axis=1, keepdims=True) + 1e-05)
    projected, kept_in = project(full_rows, section)
    projected = projected.reshape(full_rows.shape[0], 3, -1) * row_scale[:, :, None]
    gated_bf = filter_gate(projected, section, short_taps, medium_taps)
    partial_sum, kept_out = emit(gated_bf, section)
    return (combine(hidden, partial_sum), kept_in, kept_out)


def stored_project(weights_in, full_rows, section):
    chosen = lax.dynamic_index_in_dim(weights_in, section, 0, keepdims=False)
    projected = jnp.dot(
        full_rows, chosen.reshape(chosen.shape[0], -1), preferred_element_type=jnp.float32
    )
    return (projected, weights_in)


def stored_emit(weights_out, gated_bf, section):
    chosen = lax.dynamic_index_in_dim(weights_out, section, 0, keepdims=False)
    product = lax.dot_general(
        gated_bf, chosen, (((1,), (1,)), ((), ())), preferred_element_type=jnp.float32
    )
    return (product, weights_out)


def shards(stream, in_weights, out_weights, short_taps, medium_taps, plan):
    hidden = stream
    weights_in, weights_out = (
        lax.all_gather(in_weights, "ctx", axis=1, tiled=True),
        lax.all_gather(out_weights, "ctx", axis=1, tiled=True),
    )
    first_step = 0
    for step_index in range(first_step, STEPS):
        hidden, weights_in, weights_out = advance(
            hidden,
            plan[step_index],
            partial(stored_project, weights_in),
            partial(stored_emit, weights_out),
            short_taps,
            medium_taps,
        )
    return hidden


CHUNKS = 12
CROSS, MIX, DOT, MEET, UPDATE = 1, 3, 5, 7, 9
PAD = 128
LANES = 128
BF = jnp.bfloat16
F32 = jnp.float32


def wave_kernel(
    sizes, plan, stream_hbm, w_in_hbm, w_out_hbm, short_taps, medium_taps, out,
    h, w_in, w_out, taps, land, p_send, p_recv, x_send, x_recv, own, ss_own, ss_recv, mixed, gat, acc, r_send, r_recv, c_recv,
    i_r, up_s, down_s, m_s, m_r, ss_s, ss_r, p_s, p_r, x_s, x_r, g_s, g_r, r_s, r_r, c_s, c_r, b_s, b_r, o_s, o_r, w_s,
):
    tokens, rows, block, width = sizes
    ctx, chan = lax.axis_index("ctx"), lax.axis_index("chan")
    n_ctx, n_chan = 4, 4
    side, core = ctx // 2, ctx % 2
    partner = {"ctx": side * 2 + (1 - core)}
    across = {"ctx": (1 - side) * 2 + core}
    diagonal = {"ctx": (1 - side) * 2 + (1 - core)}
    relations = (partner, across, diagonal)
    last = n_chan - 1
    outer = (chan == 0) | (chan == last)
    inner = jnp.logical_not(outer)
    near = {"chan": chan + 1 - 2 * (chan % 2)}
    mid = {"chan": jnp.where(outer, near["chan"], last - chan)}
    above = {"chan": jnp.minimum(chan + 1, last)}
    below = {"chan": jnp.maximum(chan - 1, 0)}
    corner = ctx == chan
    items = STEPS * CHUNKS
    each_block = CHUNKS // n_ctx

    def remote(source, target, send, recv, device):
        return pltpu.make_async_remote_copy(
            src_ref=source, dst_ref=target, send_sem=send, recv_sem=recv,
            device_id=device, device_id_type=pl.DeviceIdType.MESH,
        )

    def span(t):
        return pl.ds(pl.multiple_of(t * rows, rows), rows)

    def lanes(index):
        return pl.ds(pl.multiple_of(index * LANES, LANES), LANES)

    def each(count, body):
        def wrapped(t, carry):
            body(t)
            return carry
        lax.fori_loop(0, count, wrapped, 0)

    barrier = pltpu.get_barrier_semaphore()

    def greet(**device):
        pl.semaphore_signal(barrier, inc=1, device_id=device, device_id_type=pl.DeviceIdType.MESH)

    for di in range(1, n_ctx):
        greet(ctx=(ctx + di) % n_ctx, chan=chan)

    @pl.when(chan < last)
    def _():
        greet(ctx=ctx, chan=chan + 1)

    @pl.when(chan > 0)
    def _():
        greet(ctx=ctx, chan=chan - 1)

    @pl.when(outer & (ctx != chan))
    def _():
        greet(ctx=chan, chan=near["chan"])

    guests = n_ctx - 1 + jnp.where(outer, 1, 2) + jnp.where(inner & (ctx == near["chan"]), n_ctx - 1, 0)
    own_load = pltpu.make_async_copy(stream_hbm, land.at[chan], w_s.at[2])
    own_load.start()
    in_load = pltpu.make_async_copy(w_in_hbm, w_in, w_s.at[0])
    out_load = pltpu.make_async_copy(w_out_hbm, w_out, w_s.at[1])
    in_load.start()
    out_load.start()
    for c in range(8):
        mixed[c, pl.ds(0, PAD), :] = jnp.zeros((PAD, LANES), F32)
    ss_own[...] = jnp.zeros(ss_own.shape, F32)
    groups, reach = medium_taps.shape
    share = LANES // (groups // n_ctx)
    row = lax.broadcasted_iota(jnp.int32, (groups, LANES), 0)
    lane = lax.broadcasted_iota(jnp.int32, (groups, LANES), 1)
    chosen = jnp.where(row == ctx * (groups // n_ctx) + lane // share, 1.0, 0.0).astype(BF)
    spread_taps = lax.dot_general(
        medium_taps[...], chosen, (((0,), (0,)), ((), ())), preferred_element_type=F32
    )
    taps[1] = spread_taps.reshape(reach // 8, 8, LANES)
    taps[0] = jnp.zeros((reach // 8, 8, LANES), F32)
    count = short_taps.shape[0]
    taps[0, 0, pl.ds(0, count), :] = short_taps[:, lanes(ctx)].astype(F32)
    pl.semaphore_wait(barrier, guests)
    own_load.wait()

    def hop_copy(source, q, j, upward):
        sems, device = (up_s, above) if upward else (down_s, below)
        return remote(source, land.at[q, span(j), :], sems.at[q, j], i_r.at[q, j], device)

    def spread_copy(source, q, j):
        chunk = ctx * each_block + j
        return remote(source, h.at[span(chunk), :], m_s.at[q, j], m_r.at[chunk], {"ctx": q})

    def keep_copy(source, j):
        chunk = ctx * each_block + j
        return pltpu.make_async_copy(source, h.at[span(chunk), :], m_r.at[chunk])

    def spread(source, q, j):
        @pl.when(q != ctx)
        def _():
            spread_copy(source, q, j).start()

        @pl.when(q == ctx)
        def _():
            keep_copy(source, j).start()

    def first(j):
        source = land.at[chan, span(j), :]

        @pl.when(chan < last)
        def _():
            hop_copy(source, chan, j, True).start()

        @pl.when(chan > 0)
        def _():
            hop_copy(source, chan, j, False).start()

        spread(source, chan, j)

    def relay(q, j, upward):
        source = land.at[q, span(j), :]
        hop_copy(source, q, j, upward).wait_recv()

        @pl.when((chan < last) if upward else (chan > 0))
        def _():
            hop_copy(source, q, j, upward).start()

        spread(source, q, j)

    def relay_round(r):
        for distance in range(last, 0, -1):
            j = r - distance
            present = (j >= 0) & (j < each_block)

            @pl.when(present & (chan >= distance))
            def _():
                relay(chan - distance, j, True)

            @pl.when(present & (chan + distance <= last))
            def _():
                relay(chan + distance, j, False)

        @pl.when(r < each_block)
        def _():
            first(r)

    def relay_settle(j):
        for q in range(n_chan):
            source = land.at[q, span(j), :]

            @pl.when((q <= chan) & (chan < last))
            def _():
                hop_copy(source, q, j, True).wait_send()

            @pl.when((q >= chan) & (chan > 0))
            def _():
                hop_copy(source, q, j, False).wait_send()

            @pl.when(q != ctx)
            def _():
                spread_copy(source, q, j).wait_send()

    def first_arrive(t):
        @pl.when(t // each_block == ctx)
        def _():
            pltpu.make_async_copy(land.at[0, span(0), :], h.at[span(t), :], m_r.at[t]).wait()

        @pl.when(t // each_block != ctx)
        def _():
            remote(land.at[0, span(0), :], h.at[span(t), :], m_s.at[0, 0], m_r.at[t], partner).wait_recv()

    def ss_copy(rel, t):
        return remote(ss_own.at[t], ss_recv.at[rel, t], ss_s.at[rel, t], ss_r.at[rel, t], relations[rel])

    def p_copy(slot, t):
        return remote(p_send.at[slot, t], p_recv.at[slot, t], p_s.at[slot, t], p_r.at[slot, t], partner)

    def x_copy(t):
        return remote(x_send.at[t], x_recv.at[t], x_s.at[t], x_r.at[t], across)

    def g_copy(rel, t, sending=True):
        ref = gat.at[span(t), lanes(ctx if sending else relations[rel]["ctx"])]
        return remote(ref, ref, g_s.at[rel, t], g_r.at[rel, t], relations[rel])

    def r_copy(t):
        return remote(r_send.at[t], r_recv.at[t], r_s.at[t], r_r.at[t], near)

    def c_copy(parity, t):
        return remote(r_send.at[t], c_recv.at[parity, t], c_s.at[parity, t], c_r.at[parity, t], mid)

    def b_copy(t):
        ref = h.at[span(t), :]
        return remote(ref, ref, b_s.at[t], b_r.at[t], near)

    home = side == chan // 2

    def gives(s):
        return inner & ((s + 1 < STEPS) | jnp.logical_not(home))

    def takes(s):
        return inner & ((s + 1 < STEPS) | home)

    def returns(s):
        return inner & (s + 1 < STEPS)

    def settle(s, t):
        for slot in range(2):
            p_copy(slot, t).wait_send()
        for rel in range(3):
            ss_copy(rel, t).wait_send()
        x_copy(t).wait_send()
        for kind in range(3):
            g_copy(kind, t).wait_send()

        @pl.when(outer)
        def _():
            r_copy(t).wait_send()

        @pl.when(gives(s))
        def _():
            c_copy(s % 2, t).wait_send()

        @pl.when(returns(s))
        def _():
            b_copy(t).wait_send()

    def project(section, t, index):
        columns = lanes(index)
        weights = jnp.concatenate([w_in[section, j, :, columns] for j in range(3)], 1)
        return jnp.dot(h[span(t), :], weights, preferred_element_type=F32)

    def enter(s, t):
        section = plan[s]

        @pl.when(s > 0)
        def _():
            settle(s - 1, t)

            @pl.when(outer)
            def _():
                b_copy(t).wait_recv()

        @pl.when(s == 0)
        def _():
            first_arrive(t)

        p_send[0, t] = project(section, t, diagonal["ctx"]).astype(BF)
        p_copy(0, t).start()
        p_send[1, t] = project(section, t, partner["ctx"]).astype(BF)
        p_copy(1, t).start()
        wide = h[span(t), :].astype(F32)
        squares = (wide * wide).astype(BF)
        ss_own[t, :, pl.ds(0, rows)] = lax.dot_general(
            jnp.ones((8, squares.shape[1]), BF), squares, (((1,), (1,)), ((), ())), preferred_element_type=F32
        )
        for rel in range(3):
            ss_copy(rel, t).start()

    def cross(s, t):
        section = plan[s]
        passing = project(section, t, across["ctx"])
        p_copy(0, t).wait_recv()
        x_send[t] = (passing + p_recv[0, t].astype(F32)).astype(BF)
        x_copy(t).start()
        own[t] = project(section, t, ctx)

    def mix(s, t):
        section = plan[s]
        for rel in range(3):
            ss_copy(rel, t).wait_recv()
        p_copy(1, t).wait_recv()
        x_copy(t).wait_recv()
        total = ss_own[t] + ss_recv[0, t] + ss_recv[1, t] + ss_recv[2, t]
        scale = lax.rsqrt(total * (1.0 / width) + 1e-05)
        scale = jnp.transpose(scale)[:rows, :1]
        parts = (own[t] + p_recv[1, t].astype(F32) + x_recv[t].astype(F32)) * scale
        query = parts[:, :LANES].astype(BF).astype(F32)
        product = parts[:, LANES:2 * LANES] * parts[:, 2 * LANES:]
        base = PAD + t * rows
        before = mixed[0, pl.ds(pl.multiple_of(base - 8, 8), 8), :]
        window = jnp.concatenate([before, product.astype(BF).astype(F32)], 0)
        for c in range(8):
            mixed[c, pl.ds(pl.multiple_of(base, rows), rows), :] = window[8 - c:8 - c + rows, :]

        def tap_block(jj, total):
            here = pl.ds(pl.multiple_of(base - 8 * jj, 8), rows)
            weights = taps[section, jj]
            for c in range(8):
                total = total + weights[c:c + 1, :] * mixed[c, here, :]
            return total

        filtered = lax.fori_loop(0, taps.shape[1], tap_block, jnp.zeros((rows, LANES), F32))
        gat[span(t), lanes(ctx)] = (query * filtered).astype(BF)
        for rel in (2, 1, 0):
            g_copy(rel, t).start()

    def dot(s, t):
        section = plan[s]
        for rel in range(3):
            g_copy(rel, t, False).wait_recv()
        product = lax.dot_general(
            gat[span(t), :], w_out[section], (((1,), (1,)), ((), ())), preferred_element_type=F32
        )

        @pl.when(outer)
        def _():
            r_send[t] = product.astype(BF)
            r_copy(t).start()

        @pl.when(inner)
        def _():
            acc[t] = product

    def meet(s, t):
        @pl.when(inner)
        def _():
            r_copy(t).wait_recv()
            r_send[t] = (acc[t] + r_recv[t].astype(F32)).astype(BF)

        @pl.when(gives(s))
        def _():
            c_copy(s % 2, t).start()

    def out_copy(t):
        there = span(t % each_block)
        return remote(
            h.at[span(t), :], out.at[there, :], o_s.at[t], o_r.at[t % each_block],
            {"ctx": t // each_block, "chan": ctx},
        )

    def keep_out(t):
        there = span(t % each_block)
        return pltpu.make_async_copy(h.at[span(t), :], out.at[there, :], o_s.at[t])

    def stays(t):
        return corner & (t // each_block == ctx)

    def update(s, t):
        @pl.when(takes(s))
        def _():
            parity = s % 2
            c_copy(parity, t).wait_recv()
            total = r_send[t].astype(F32) + c_recv[parity, t].astype(F32)
            h[span(t), :] = (h[span(t), :].astype(F32) + total).astype(BF)

        @pl.when(returns(s))
        def _():
            b_copy(t).start()

        @pl.when((s + 1 == STEPS) & inner & home & jnp.logical_not(stays(t)))
        def _():
            out_copy(t).start()

        @pl.when((s + 1 == STEPS) & inner & home & stays(t))
        def _():
            keep_out(t).start()

    stages = (
        (CROSS, cross), (UPDATE, update), (MEET, meet), (DOT, dot), (MIX, mix), (0, enter),
    )

    def tick(u):
        for lag, body in stages:
            @pl.when((u >= lag) & (u < items + lag))
            def _():
                n = u - lag
                body(n // CHUNKS, n % CHUNKS)

        @pl.when((core == 0) & (u < each_block - 1))
        def _():
            relay_round(last + 1 + u)

        @pl.when((core == 1) & (u < 2))
        def _():
            relay_round(u)

        @pl.when((core == 1) & (u >= 2) & (u < 2 + each_block // 2 + 1))
        def _():
            for extra in range(2):
                relay_round(2 * u - 2 + extra)

    @pl.when(core == 0)
    def _():
        each(last + 1, relay_round)

    in_load.wait()
    out_load.wait()
    each(items + UPDATE, tick)

    def finish(t):
        settle(STEPS - 1, t)

        @pl.when(inner & home & jnp.logical_not(stays(t)))
        def _():
            out_copy(t).wait_send()

        @pl.when(inner & home & stays(t))
        def _():
            keep_out(t).wait()

    each(CHUNKS, finish)

    def received(j):
        relay_settle(j)

        @pl.when(jnp.logical_not(corner & inner))
        def _():
            out_copy(j).wait_recv()

    each(each_block, received)


def wave(stream, in_weights, out_weights, short_taps, medium_taps, plan):
    n_ctx = lax.axis_size("ctx")
    n_chan = lax.axis_size("chan")
    features, channels = in_weights.shape[1], in_weights.shape[3]
    tokens = stream.shape[0] * n_ctx
    rows = tokens // CHUNKS
    each_block = CHUNKS // n_ctx
    block = 3 * LANES
    reach = medium_taps.shape[0]
    w_in = in_weights.transpose(0, 2, 1, 3)
    vmem = pl.BlockSpec(memory_space=pltpu.VMEM)
    anywhere = pl.BlockSpec(memory_space=pl.ANY)
    dma = pltpu.SemaphoreType.DMA
    scratch = [
        pltpu.VMEM((tokens, features), BF),
        pltpu.VMEM(w_in.shape, BF),
        pltpu.VMEM(out_weights.shape, BF),
        pltpu.VMEM((2, reach // 8, 8, LANES), F32),
        pltpu.VMEM((n_chan, stream.shape[0], features), BF),
        pltpu.VMEM((2, CHUNKS, rows, block), BF),
        pltpu.VMEM((2, CHUNKS, rows, block), BF),
        pltpu.VMEM((CHUNKS, rows, block), BF),
        pltpu.VMEM((CHUNKS, rows, block), BF),
        pltpu.VMEM((CHUNKS, rows, block), F32),
        pltpu.VMEM((CHUNKS, 8, LANES), F32),
        pltpu.VMEM((3, CHUNKS, 8, LANES), F32),
        pltpu.VMEM((8, PAD + tokens, LANES), F32),
        pltpu.VMEM((tokens, channels), BF),
        pltpu.VMEM((CHUNKS, rows, features), F32),
        pltpu.VMEM((CHUNKS, rows, features), BF),
        pltpu.VMEM((CHUNKS, rows, features), BF),
        pltpu.VMEM((2, CHUNKS, rows, features), BF),
        dma((n_chan, each_block)), dma((n_chan, each_block)), dma((n_chan, each_block)),
        dma((n_chan, each_block)), dma((CHUNKS,)),
        dma((3, CHUNKS)), dma((3, CHUNKS)),
        dma((2, CHUNKS)), dma((2, CHUNKS)),
        dma((CHUNKS,)), dma((CHUNKS,)),
        dma((3, CHUNKS)), dma((3, CHUNKS)),
        dma((CHUNKS,)), dma((CHUNKS,)),
        dma((2, CHUNKS)), dma((2, CHUNKS)),
        dma((CHUNKS,)), dma((CHUNKS,)),
        dma((CHUNKS,)), dma((each_block,)), dma((3,)),
    ]
    sizes = (tokens, rows, block, features * n_ctx)
    return pl.pallas_call(
        partial(wave_kernel, sizes),
        out_shape=jax.ShapeDtypeStruct(stream.shape, stream.dtype),
        in_specs=[pl.BlockSpec(memory_space=pltpu.SMEM), anywhere, anywhere, anywhere, vmem, vmem],
        out_specs=anywhere,
        scratch_shapes=scratch,
        compiler_params=pltpu.CompilerParams(
            collective_id=0, has_side_effects=True, vmem_limit_bytes=60 * 1024 * 1024
        ),
    )(plan, stream, w_in, out_weights, short_taps, medium_taps.T)


def fits(mesh, stream, in_weights, medium_taps):
    n_ctx, n_chan = mesh.shape["ctx"], mesh.shape["chan"]
    tokens = stream.shape[0] // mesh.shape["groups"]
    channels = in_weights.shape[3] // n_chan
    return (
        n_ctx == 4 and n_chan == 4 and channels == n_ctx * LANES
        and stream.shape[1] // n_chan == in_weights.shape[1] // n_ctx
        and tokens == 768 and medium_taps.shape[0] == PAD
    )


def solution(mesh):
    def run(stream, in_weights, out_weights, short_taps, medium_taps, plan):
        body = wave if fits(mesh, stream, in_weights, medium_taps) else shards
        return jax.shard_map(
            body,
            mesh=mesh,
            in_specs=(
                P(("groups", "ctx"), "chan"),
                P(None, "ctx", None, "chan"),
                P(None, "ctx", "chan"),
                P(None, "chan"),
                P(None, "chan"),
                P(),
            ),
            out_specs=P(("groups", "ctx"), "chan"),
            check_vma=False,
        )(stream, in_weights, out_weights, short_taps, medium_taps, plan)

    return run
```
